32 devices in a mesh: tok: 4 (over z), feat: 8 (over y, x, core).
Axes of the slice: x: 2, y: 2, z: 4, core: 2. Of those that a mesh axis runs over, the one named last changes fastest.
Arguments:
- activations: float32 [1024, 8192], P('tok', 'feat'), may hold values from -40 to 40
- gradients: float32 [1024, 28672], P('tok', 'feat'), may hold values from -40 to 40
- input_basis: float32 [8192, 8192], P('feat', 'tok'), may hold values from -0.09375 to 0.09375
- output_basis: float32 [28672, 1792], P('feat', 'tok'), may hold values from -0.046875 to 0.046875
Outputs:
- eigenvalues: float32 [8192, 1792], P('tok', 'feat')
The draws below stay inside these ranges and needn't reach their ends.
All inputs are finite; a program needn't handle non-finite values.
Results may differ from the reference program's by a relative error of at most 0.00016.
Values sent between devices are 32-bit elements; how exact they have to be, the bound alone decides.
A program may use at most 128 MiB of HBM per device.

```python
import jax
import jax.numpy as jnp
from jax import lax

D = 8192
DOUT = 28672
WINDOW = 1792
TOKENS = 1024


def token_matrix(key, count, width):
    noise = jnp.clip(jax.random.normal(jax.random.fold_in(key, 11), (count, width), jnp.float32), -6.0, 6.0)
    ramp = 1.0 + 2.0 * jnp.arange(count, dtype=jnp.float32) / (count - 1)
    rough = jnp.exp(jax.random.uniform(jax.random.fold_in(key, 14), (count,), jnp.float32, -0.35, 0.35))
    factor = 0.6 * ramp * rough
    return noise * factor[:, None]


def draw_activations(key, part):
    return token_matrix(jax.random.fold_in(key, 101), TOKENS, D)


def draw_gradients(key, part):
    return token_matrix(jax.random.fold_in(key, 202), TOKENS, DOUT)


def with_spikes(values, key, source, target, parts, factor):
    def block_of(position):
        return (jnp.arange(values.shape[position]) // (values.shape[position] // parts)).reshape((-1,) + (1,) * (values.ndim - 1 - position))

    first = jax.random.permutation(key, parts)[block_of(target)]
    other_side = (block_of(target) + parts // 2) % parts
    return jnp.where((block_of(source) == first) | (block_of(source) == other_side), factor * values, values)


def level_of(rng, dims, split, least, top_value):
    loudness, own = 1.0, jax.random.fold_in(rng, 6)
    for axis_at, blocks in split:
        steps = jnp.exp(jax.random.uniform(jax.random.fold_in(own, axis_at), (blocks,), jnp.float32, least / len(split), top_value / len(split)))
        loudness = loudness * jnp.repeat(steps, dims[axis_at] // blocks).reshape([-1 if axis == axis_at else 1 for axis in range(len(dims))])
    return loudness


def bell_draw_with(own_key, extent, scale, reach, cuts, heavy, held_as=jnp.bfloat16):
    entries = scale * jax.random.normal(own_key, extent, jnp.float32)
    if cuts:
        entries = entries * level_of(own_key, extent, cuts, -0.22, 0.18)
    return jnp.clip(with_spikes(entries, jax.random.fold_in(own_key, 3), *heavy), -reach, reach).astype(held_as)


def setup_inputs(seed: int = 0) -> dict:
    splits = jax.random.split(jax.random.key(seed), 5)
    activations = draw_activations(jax.random.fold_in(splits[4], 71), 0)
    gradients = draw_gradients(jax.random.fold_in(splits[4], 71), 0)
    input_basis = bell_draw_with(splits[2], (D, D), D ** -0.5, 0.09375, ((0, 8), (1, 4)), (0, 1, 8, 2.0), jnp.float32)
    output_basis = bell_draw_with(splits[3], (DOUT, WINDOW), DOUT ** -0.5, 0.046875, ((0, 8), (1, 4)), (0, 1, 8, 2.0), jnp.float32)
    return dict(activations=activations, gradients=gradients, input_basis=input_basis, output_basis=output_basis)


def reference(activations, gradients, input_basis, output_basis):
    highest = lax.Precision.HIGHEST
    input_coords = jnp.dot(activations, input_basis, precision=highest, preferred_element_type=jnp.float32)
    output_coords = jnp.dot(gradients, output_basis, precision=highest, preferred_element_type=jnp.float32)
    input_squares = input_coords * input_coords
    output_squares = output_coords * output_coords
    summed = jnp.dot(input_squares.T, output_squares, precision=highest, preferred_element_type=jnp.float32)
    return summed / TOKENS
```

```python
import jax
import jax.numpy as jnp
from jax import lax
from jax.sharding import PartitionSpec as P


def dot3(left, right):
    return jnp.dot(left, right, precision=lax.Precision.HIGH, preferred_element_type=jnp.float32)


def line_gather(block, place, count):
    up, down = [block], [block]
    for hop in range(1, count):
        up.append(lax.ppermute(up[-1], "tok", [(i, i + 1) for i in range(hop - 1, count - 1)]))
        down.append(lax.ppermute(down[-1], "tok", [(i, i - 1) for i in range(1, count - hop + 1)]))
    return [block] + [
        jnp.where(place + hop < count, down[hop], up[count - hop]) for hop in range(1, count)
    ]


def per_device(count, feats, activations, gradients, input_basis, output_basis):
    place = lax.axis_index("tok")
    total_tokens = activations.shape[0] * count
    depth = gradients.shape[1]
    inner = count == 4
    first = depth // 2 if inner else depth

    inputs = line_gather(activations, place, count)
    input_partial = jnp.concatenate([dot3(block, input_basis) for block in inputs])
    input_coords = lax.psum_scatter(input_partial, "feat", scatter_dimension=0, tiled=True)
    input_squares = input_coords * input_coords

    outputs = line_gather(gradients[:, :first], place, count)
    if inner:
        rest, rest_basis = gradients[:, first:], output_basis[first:]
        outer_basis = lax.ppermute(rest_basis, "tok", [(0, 1), (3, 2)])
        below = lax.ppermute(rest, "tok", [(0, 1), (1, 2)])
        above = lax.ppermute(rest, "tok", [(3, 2), (2, 1)])
        across = lax.ppermute(jnp.where(place == 1, below, above), "tok", [(1, 2), (2, 1)])
        middle = (place == 1) | (place == 2)
        blocks = [rest, above, across, below]
    input_squares, outputs[-1], outputs[-2] = lax.optimization_barrier(
        (input_squares, outputs[-1], outputs[-2])
    )
    all_inputs = lax.all_gather(input_squares, "feat", axis=0, tiled=True)
    partials = [dot3(block, output_basis[:first]) for block in outputs]
    rows = activations.shape[0]

    def in_order(parts):
        return jnp.roll(jnp.concatenate(parts), place * rows, axis=0)

    if inner:
        partials = [
            part + jnp.where(middle, dot3(block, rest_basis), 0.0)
            for part, block in zip(partials, blocks)
        ]
        others = in_order([dot3(block, outer_basis) for block in blocks])
        others = lax.psum_scatter(others, "feat", scatter_dimension=0, tiled=True)
        output_coords = lax.psum_scatter(in_order(partials), "feat", scatter_dimension=0, tiled=True)
        output_coords = output_coords + lax.ppermute(others, "tok", [(1, 0), (2, 3)])
    else:
        output_coords = lax.psum_scatter(in_order(partials), "feat", scatter_dimension=0, tiled=True)
    output_squares = output_coords * output_coords
    every_square = lax.all_gather(output_squares, "tok", axis=1, tiled=True)
    own_square = lax.all_to_all(every_square, "feat", split_axis=1, concat_axis=0, tiled=True)
    own_square = jnp.roll(own_square, -place * rows, axis=0)
    summed = lax.dot_general(
        all_inputs,
        own_square,
        (((0,), (0,)), ((), ())),
        precision=lax.Precision.HIGH,
        preferred_element_type=jnp.float32,
    )
    return summed / total_tokens


def solution(mesh):
    count, feats = mesh.shape["tok"], mesh.shape["feat"]
    in_specs = (P("tok", "feat"), P("tok", "feat"), P("feat", "tok"), P("feat", "tok"))
    out_specs = P("tok", "feat")

    def body(*args):
        return per_device(count, feats, *args)

    return jax.shard_map(body, mesh=mesh, in_specs=in_specs, out_specs=out_specs, check_vma=False)
```

```python
import functools

import jax
import jax.numpy as jnp
from jax import lax
from jax.experimental import pallas as pl
from jax.experimental.pallas import tpu as pltpu
from jax.sharding import PartitionSpec as P


def dot3(left, right):
    return jnp.dot(left, right, precision=lax.Precision.HIGH, preferred_element_type=jnp.float32)


def line_gather(block, place, count):
    up, down = [block], [block]
    for hop in range(1, count):
        up.append(lax.ppermute(up[-1], "tok", [(i, i + 1) for i in range(hop - 1, count - 1)]))
        down.append(lax.ppermute(down[-1], "tok", [(i, i - 1) for i in range(1, count - hop + 1)]))
    return [block] + [
        jnp.where(place + hop < count, down[hop], up[count - hop]) for hop in range(1, count)
    ]


PIECES = 4
MESH = pl.DeviceIdType.MESH


def exchange_kernel(first, grads, basis, near, far, outer, near_recv, near_up, near_down, far_recv, far_send, extra):
    place = lax.axis_index("tok")
    rows = grads.shape[0]
    step = rows // PIECES
    rest = grads.shape[1] - first

    def near_copy(src, piece, own, target, sems):
        at = pl.ds(piece * step, step)
        source = grads.at[at, pl.ds(0, first)] if own else near.at[src, at, :]
        return pltpu.make_async_remote_copy(
            src_ref=source,
            dst_ref=near.at[src, at, :],
            send_sem=sems.at[src, piece],
            recv_sem=near_recv.at[src, piece],
            device_id={"tok": target},
            device_id_type=MESH,
        )

    def far_copy(src, piece, own, target):
        at = pl.ds(piece * step, step)
        source = grads.at[at, pl.ds(first, rest)] if own else far.at[src, at, :]
        return pltpu.make_async_remote_copy(
            src_ref=source,
            dst_ref=far.at[src, at, :],
            send_sem=far_send.at[src, piece],
            recv_sem=far_recv.at[src, piece],
            device_id={"tok": target},
            device_id_type=MESH,
        )

    def outer_copy(target):
        return pltpu.make_async_remote_copy(
            src_ref=basis.at[:, pl.ds(first, rest)],
            dst_ref=outer,
            send_sem=extra.at[0],
            recv_sem=extra.at[1],
            device_id={"tok": target},
            device_id_type=MESH,
        )

    barrier = pltpu.get_barrier_semaphore()

    def role(me):
        neighbours = [p for p in (me - 1, me + 1) if 0 <= p < 4]
        inner = me in (1, 2)
        for p in neighbours:
            pl.semaphore_signal(barrier, inc=1, device_id={"tok": p}, device_id_type=MESH)
        pl.semaphore_wait(barrier, len(neighbours))

        sent = []

        def send(copy):
            copy.start()
            sent.append(copy)

        kept = [pltpu.make_async_copy(grads.at[:, pl.ds(0, first)], near.at[me], extra.at[2])]
        if inner:
            kept.append(pltpu.make_async_copy(grads.at[:, pl.ds(first, rest)], far.at[me], extra.at[3]))
        mate = {0: 1, 1: 2, 2: 1, 3: 2}[me]
        for piece in range(PIECES):
            if me < 3:
                send(near_copy(me, piece, True, me + 1, near_up))
            if me > 0:
                send(near_copy(me, piece, True, me - 1, near_down))
        for piece in range(PIECES):
            send(far_copy(me, piece, True, mate))
        if not inner:
            send(outer_copy(mate))
        for copy in kept:
            copy.start()

        def take_near(src, piece):
            near_copy(src, piece, False, mate, near_up).wait_recv()
            if src < me < 3:
                send(near_copy(src, piece, False, me + 1, near_up))
            if 0 < me < src:
                send(near_copy(src, piece, False, me - 1, near_down))

        def take_far(src, piece):
            far_copy(src, piece, False, mate).wait_recv()
            if (me, src) in ((1, 0), (2, 3)):
                send(far_copy(src, piece, False, mate))

        for hop in (1, 2, 3):
            for piece in range(PIECES):
                for src in (me - hop, me + hop):
                    if 0 <= src < 4:
                        take_near(src, piece)
            if inner and hop == 1:
                for piece in range(PIECES):
                    take_far(0 if me == 1 else 3, piece)
        if inner:
            for src in (2, 3) if me == 1 else (1, 0):
                for piece in range(PIECES):
                    take_far(src, piece)
            outer_copy(mate).wait_recv()
        for copy in sent:
            copy.wait_send()
        for copy in kept:
            copy.wait()

    for me in range(4):
        pl.when(place == me)(functools.partial(role, me))


def exchange(first, gradients, basis):
    rows, depth = gradients.shape
    rest = depth - first
    pieces = pltpu.SemaphoreType.DMA((4, PIECES))
    return pl.pallas_call(
        functools.partial(exchange_kernel, first),
        out_shape=(
            jax.ShapeDtypeStruct((4, rows, first), gradients.dtype),
            jax.ShapeDtypeStruct((4, rows, rest), gradients.dtype),
            jax.ShapeDtypeStruct((basis.shape[0], rest), basis.dtype),
        ),
        in_specs=[pl.BlockSpec(memory_space=pl.ANY)] * 2,
        out_specs=(pl.BlockSpec(memory_space=pl.ANY),) * 3,
        scratch_shapes=[pieces] * 5 + [pltpu.SemaphoreType.DMA((4,))],
        cost_estimate=pl.CostEstimate(flops=100_000_000_000, bytes_accessed=100_000_000, transcendentals=0),
        compiler_params=pltpu.CompilerParams(collective_id=1, has_side_effects=True),
    )(gradients, basis)


def per_device(count, feats, activations, gradients, input_basis, output_basis):
    place = lax.axis_index("tok")
    total_tokens = activations.shape[0] * count
    depth = gradients.shape[1]
    inner = count == 4
    first = depth // 2 if inner else depth

    inputs = line_gather(activations, place, count)
    input_partial = jnp.concatenate([dot3(block, input_basis) for block in inputs])
    if inner:
        gradients, input_partial = lax.optimization_barrier((gradients, input_partial))
        all_inputs = lax.psum(input_partial, "feat")
        near, far, outer_basis = exchange(first, gradients, output_basis.T)
        all_inputs, near, far = lax.optimization_barrier((all_inputs, near, far))
        middle = (place == 1) | (place == 2)
        near, far = near.reshape(total_tokens, -1), far.reshape(total_tokens, -1)
        partial = dot3(near, output_basis[:first])
        partial = partial + jnp.where(middle, dot3(far, output_basis[first:]), 0.0)
        others = dot3(far, outer_basis.T)
        others = lax.psum_scatter(others, "feat", scatter_dimension=0, tiled=True)
        output_coords = lax.psum_scatter(partial, "feat", scatter_dimension=0, tiled=True)
        output_coords = output_coords + lax.ppermute(others, "tok", [(1, 0), (2, 3)])
    else:
        all_inputs = lax.psum(input_partial, "feat")
        outputs = line_gather(gradients, place, count)
        partial = jnp.concatenate([dot3(block, output_basis) for block in outputs])
        partial = jnp.roll(partial, place * activations.shape[0], axis=0)
        output_coords = lax.psum_scatter(partial, "feat", scatter_dimension=0, tiled=True)
    output_squares = output_coords * output_coords
    every_square = lax.all_gather(output_squares, "tok", axis=1, tiled=True)
    own_square = lax.all_to_all(every_square, "feat", split_axis=1, concat_axis=0, tiled=True)
    own_square = jnp.roll(own_square, -place * activations.shape[0], axis=0)
    summed = lax.dot_general(
        all_inputs * all_inputs,
        own_square,
        (((0,), (0,)), ((), ())),
        precision=lax.Precision.HIGH,
        preferred_element_type=jnp.float32,
    )
    return summed / total_tokens


def solution(mesh):
    count, feats = mesh.shape["tok"], mesh.shape["feat"]
    in_specs = (P("tok", "feat"), P("tok", "feat"), P("feat", "tok"), P("feat", "tok"))
    out_specs = P("tok", "feat")

    def body(*args):
        return per_device(count, feats, *args)

    return jax.shard_map(body, mesh=mesh, in_specs=in_specs, out_specs=out_specs, check_vma=False)
```

```python
import functools

import jax
import jax.numpy as jnp
from jax import lax
from jax.experimental import pallas as pl
from jax.experimental.pallas import tpu as pltpu
from jax.sharding import PartitionSpec as P


def dot3(left, right):
    return jnp.dot(left, right, precision=lax.Precision.HIGH, preferred_element_type=jnp.float32)


def line_gather(block, place, count):
    up, down = [block], [block]
    for hop in range(1, count):
        up.append(lax.ppermute(up[-1], "tok", [(i, i + 1) for i in range(hop - 1, count - 1)]))
        down.append(lax.ppermute(down[-1], "tok", [(i, i - 1) for i in range(1, count - hop + 1)]))
    blocks = [block] + [
        jnp.where(place + hop < count, down[hop], up[count - hop]) for hop in range(1, count)
    ]
    return blocks, (up[count // 2], down[count // 2])


PIECES = 4
MESH = pl.DeviceIdType.MESH


def exchange_kernel(first, grads, near, far, near_recv, near_up, near_down, far_recv, far_send, extra):
    place = lax.axis_index("tok")
    rows = grads.shape[0]
    step = rows // PIECES
    rest = grads.shape[1] - first

    def near_copy(src, piece, own, target, sems):
        at = pl.ds(piece * step, step)
        source = grads.at[at, pl.ds(0, first)] if own else near.at[src, at, :]
        return pltpu.make_async_remote_copy(
            src_ref=source,
            dst_ref=near.at[src, at, :],
            send_sem=sems.at[src, piece],
            recv_sem=near_recv.at[src, piece],
            device_id={"tok": target},
            device_id_type=MESH,
        )

    def far_copy(src, piece, own, target):
        at = pl.ds(piece * step, step)
        source = grads.at[at, pl.ds(first, rest)] if own else far.at[src, at, :]
        return pltpu.make_async_remote_copy(
            src_ref=source,
            dst_ref=far.at[src, at, :],
            send_sem=far_send.at[src, piece],
            recv_sem=far_recv.at[src, piece],
            device_id={"tok": target},
            device_id_type=MESH,
        )

    barrier = pltpu.get_barrier_semaphore()

    def role(me):
        neighbours = [p for p in (me - 1, me + 1) if 0 <= p < 4]
        inner = me in (1, 2)
        for p in neighbours:
            pl.semaphore_signal(barrier, inc=1, device_id={"tok": p}, device_id_type=MESH)
        pl.semaphore_wait(barrier, len(neighbours))

        sent = []

        def send(copy):
            copy.start()
            sent.append(copy)

        kept = pltpu.make_async_copy(grads.at[:, pl.ds(0, first)], near.at[me], extra.at[0])
        mate = {0: 1, 1: 2, 2: 1, 3: 2}[me]
        for piece in range(PIECES):
            if me < 3:
                send(near_copy(me, piece, True, me + 1, near_up))
            if me > 0:
                send(near_copy(me, piece, True, me - 1, near_down))
        if not inner:
            for piece in range(PIECES):
                send(far_copy(me, piece, True, mate))
        kept.start()

        def take_near(src, piece):
            near_copy(src, piece, False, mate, near_up).wait_recv()
            if src < me < 3:
                send(near_copy(src, piece, False, me + 1, near_up))
            if 0 < me < src:
                send(near_copy(src, piece, False, me - 1, near_down))

        def take_far(src, piece):
            far_copy(src, piece, False, mate).wait_recv()
            if (me, src) in ((1, 0), (2, 3)):
                send(far_copy(src, piece, False, mate))

        for hop in (1, 2, 3):
            for piece in range(PIECES):
                for src in (me - hop, me + hop):
                    if 0 <= src < 4:
                        take_near(src, piece)
            if inner and hop == 1:
                for piece in range(PIECES):
                    take_far(0 if me == 1 else 3, piece)
        if inner:
            for piece in range(PIECES):
                take_far(3 if me == 1 else 0, piece)
        for copy in sent:
            copy.wait_send()
        kept.wait()

    for me in range(4):
        pl.when(place == me)(functools.partial(role, me))


def exchange(first, gradients):
    rows, depth = gradients.shape
    rest = depth - first
    pieces = pltpu.SemaphoreType.DMA((4, PIECES))
    return pl.pallas_call(
        functools.partial(exchange_kernel, first),
        out_shape=(
            jax.ShapeDtypeStruct((4, rows, first), gradients.dtype),
            jax.ShapeDtypeStruct((4, rows, rest), gradients.dtype),
        ),
        in_specs=[pl.BlockSpec(memory_space=pl.ANY)],
        out_specs=(pl.BlockSpec(memory_space=pl.ANY),) * 2,
        scratch_shapes=[pieces] * 5 + [pltpu.SemaphoreType.DMA((1,))],
        cost_estimate=pl.CostEstimate(flops=100_000_000_000, bytes_accessed=100_000_000, transcendentals=0),
        compiler_params=pltpu.CompilerParams(collective_id=1, has_side_effects=True),
    )(gradients)


def per_device(count, feats, activations, gradients, input_basis, output_basis):
    place = lax.axis_index("tok")
    total_tokens = activations.shape[0] * count
    depth = gradients.shape[1]
    inner = count == 4
    first = depth // 2 if inner else depth

    inputs, landed = line_gather(activations, place, count)
    input_partial = jnp.concatenate([dot3(block, input_basis) for block in inputs])
    if inner:
        outer_basis = lax.ppermute(output_basis[first:], "tok", [(0, 1), (3, 2)])
        rest, _ = lax.optimization_barrier((gradients[:, first:], landed))
        across = lax.ppermute(rest, "tok", [(1, 2), (2, 1)])
        gradients, input_partial = lax.optimization_barrier((gradients, input_partial))
        all_inputs = lax.psum(input_partial, "feat")
        near, far = exchange(first, gradients)
        all_inputs, near, far = lax.optimization_barrier((all_inputs, near, far))
        middle = (place == 1) | (place == 2)
        far = lax.dynamic_update_index_in_dim(far, rest, place, 0)
        far = lax.dynamic_update_index_in_dim(far, across, count - 1 - place, 0)
        near, far = near.reshape(total_tokens, -1), far.reshape(total_tokens, -1)
        partial = dot3(near, output_basis[:first])
        partial = partial + jnp.where(middle, dot3(far, output_basis[first:]), 0.0)
        others = dot3(far, outer_basis)
        others = lax.psum_scatter(others, "feat", scatter_dimension=0, tiled=True)
        output_coords = lax.psum_scatter(partial, "feat", scatter_dimension=0, tiled=True)
        output_coords = output_coords + lax.ppermute(others, "tok", [(1, 0), (2, 3)])
    else:
        all_inputs = lax.psum(input_partial, "feat")
        outputs, _ = line_gather(gradients, place, count)
        partial = jnp.concatenate([dot3(block, output_basis) for block in outputs])
        partial = jnp.roll(partial, place * activations.shape[0], axis=0)
        output_coords = lax.psum_scatter(partial, "feat", scatter_dimension=0, tiled=True)
    output_squares = output_coords * output_coords
    every_square = lax.all_gather(output_squares, "tok", axis=1, tiled=True)
    own_square = lax.all_to_all(every_square, "feat", split_axis=1, concat_axis=0, tiled=True)
    own_square = jnp.roll(own_square, -place * activations.shape[0], axis=0)
    summed = lax.dot_general(
        all_inputs * all_inputs,
        own_square,
        (((0,), (0,)), ((), ())),
        precision=lax.Precision.HIGH,
        preferred_element_type=jnp.float32,
    )
    return summed / total_tokens


def solution(mesh):
    count, feats = mesh.shape["tok"], mesh.shape["feat"]
    in_specs = (P("tok", "feat"), P("tok", "feat"), P("feat", "tok"), P("feat", "tok"))
    out_specs = P("tok", "feat")

    def body(*args):
        return per_device(count, feats, *args)

    return jax.shard_map(body, mesh=mesh, in_specs=in_specs, out_specs=out_specs, check_vma=False)
```

```python
import functools

import jax
import jax.numpy as jnp
from jax import lax
from jax.experimental import pallas as pl
from jax.experimental.pallas import tpu as pltpu
from jax.sharding import PartitionSpec as P


def dot3(left, right):
    return jnp.dot(left, right, precision=lax.Precision.HIGH, preferred_element_type=jnp.float32)


def line_gather(block, place, count):
    up, down = [block], [block]
    for hop in range(1, count):
        up.append(lax.ppermute(up[-1], "tok", [(i, i + 1) for i in range(hop - 1, count - 1)]))
        down.append(lax.ppermute(down[-1], "tok", [(i, i - 1) for i in range(1, count - hop + 1)]))
    blocks = [block] + [
        jnp.where(place + hop < count, down[hop], up[count - hop]) for hop in range(1, count)
    ]
    return blocks, (up[count // 2], down[count // 2])


PIECES = 4
MESH = pl.DeviceIdType.MESH


def exchange_kernel(first, grads, near, far, near_recv, near_up, near_down, far_recv, far_send, extra):
    place = lax.axis_index("tok")
    rows = grads.shape[0]
    step = rows // PIECES
    rest = grads.shape[1] - first

    def near_copy(src, piece, own, target, sems):
        at = pl.ds(piece * step, step)
        source = grads.at[at, pl.ds(0, first)] if own else near.at[src, at, :]
        return pltpu.make_async_remote_copy(
            src_ref=source,
            dst_ref=near.at[src, at, :],
            send_sem=sems.at[src, piece],
            recv_sem=near_recv.at[src, piece],
            device_id={"tok": target},
            device_id_type=MESH,
        )

    def far_copy(src, piece, own, target):
        at = pl.ds(piece * step, step)
        source = grads.at[at, pl.ds(first, rest)] if own else far.at[src, at, :]
        return pltpu.make_async_remote_copy(
            src_ref=source,
            dst_ref=far.at[src, at, :],
            send_sem=far_send.at[src, piece],
            recv_sem=far_recv.at[src, piece],
            device_id={"tok": target},
            device_id_type=MESH,
        )

    barrier = pltpu.get_barrier_semaphore()

    def role(me):
        neighbours = [p for p in (me - 1, me + 1) if 0 <= p < 4]
        inner = me in (1, 2)
        for p in neighbours:
            pl.semaphore_signal(barrier, inc=1, device_id={"tok": p}, device_id_type=MESH)
        pl.semaphore_wait(barrier, len(neighbours))

        sent = []

        def send(copy):
            copy.start()
            sent.append(copy)

        kept = pltpu.make_async_copy(grads.at[:, pl.ds(0, first)], near.at[me], extra.at[0])
        mate = {0: 1, 1: 2, 2: 1, 3: 2}[me]
        for piece in range(PIECES):
            if me < 3:
                send(near_copy(me, piece, True, me + 1, near_up))
            if me > 0:
                send(near_copy(me, piece, True, me - 1, near_down))
        if not inner:
            for piece in range(PIECES):
                send(far_copy(me, piece, True, mate))
        kept.start()

        def take_near(src, piece):
            near_copy(src, piece, False, mate, near_up).wait_recv()
            if src < me < 3:
                send(near_copy(src, piece, False, me + 1, near_up))
            if 0 < me < src:
                send(near_copy(src, piece, False, me - 1, near_down))

        def take_far(src, piece):
            far_copy(src, piece, False, mate).wait_recv()
            if (me, src) in ((1, 0), (2, 3)):
                send(far_copy(src, piece, False, mate))

        for hop in (1, 2, 3):
            for piece in range(PIECES):
                for src in (me - hop, me + hop):
                    if 0 <= src < 4:
                        take_near(src, piece)
            if inner and hop == 1:
                for piece in range(PIECES):
                    take_far(0 if me == 1 else 3, piece)
        if inner:
            for piece in range(PIECES):
                take_far(3 if me == 1 else 0, piece)
        for copy in sent:
            copy.wait_send()
        kept.wait()

    for me in range(4):
        pl.when(place == me)(functools.partial(role, me))


def exchange(first, gradients):
    rows, depth = gradients.shape
    rest = depth - first
    pieces = pltpu.SemaphoreType.DMA((4, PIECES))
    return pl.pallas_call(
        functools.partial(exchange_kernel, first),
        out_shape=(
            jax.ShapeDtypeStruct((4, rows, first), gradients.dtype),
            jax.ShapeDtypeStruct((4, rows, rest), gradients.dtype),
        ),
        in_specs=[pl.BlockSpec(memory_space=pl.ANY)],
        out_specs=(pl.BlockSpec(memory_space=pl.ANY),) * 2,
        scratch_shapes=[pieces] * 5 + [pltpu.SemaphoreType.DMA((1,))],
        cost_estimate=pl.CostEstimate(flops=100_000_000_000, bytes_accessed=100_000_000, transcendentals=0),
        compiler_params=pltpu.CompilerParams(collective_id=1, has_side_effects=True),
    )(gradients)


def per_device(count, feats, activations, gradients, input_basis, output_basis):
    place = lax.axis_index("tok")
    total_tokens = activations.shape[0] * count
    depth = gradients.shape[1]
    inner = count == 4
    first = depth // 2 if inner else depth

    inputs, landed = line_gather(activations, place, count)
    input_partial = jnp.concatenate([dot3(block, input_basis) for block in inputs])
    if inner:
        outer_basis = lax.ppermute(output_basis[first:], "tok", [(0, 1), (3, 2)])
        rest, _ = lax.optimization_barrier((gradients[:, first:], landed))
        across = lax.ppermute(rest, "tok", [(1, 2), (2, 1)])
        gradients, input_partial = lax.optimization_barrier((gradients, input_partial))
        all_inputs = lax.psum(input_partial, "feat")
        near, far = exchange(first, gradients)
        all_inputs, near, far = lax.optimization_barrier((all_inputs, near, far))
        middle = (place == 1) | (place == 2)
        far = lax.dynamic_update_index_in_dim(far, rest, place, 0)
        far = lax.dynamic_update_index_in_dim(far, across, count - 1 - place, 0)
        near, far = near.reshape(total_tokens, -1), far.reshape(total_tokens, -1)
        partial = dot3(near, output_basis[:first])
        partial = partial + jnp.where(middle, dot3(far, output_basis[first:]), 0.0)
        others = dot3(far, outer_basis)
        both = jnp.concatenate([partial, others], axis=1)
        both = lax.psum_scatter(both, "feat", scatter_dimension=0, tiled=True)
        width = partial.shape[1]
        output_coords = both[:, :width] + lax.ppermute(both[:, width:], "tok", [(1, 0), (2, 3)])
    else:
        all_inputs = lax.psum(input_partial, "feat")
        outputs, _ = line_gather(gradients, place, count)
        partial = jnp.concatenate([dot3(block, output_basis) for block in outputs])
        partial = jnp.roll(partial, place * activations.shape[0], axis=0)
        output_coords = lax.psum_scatter(partial, "feat", scatter_dimension=0, tiled=True)
    output_squares = output_coords * output_coords
    every_square = lax.all_gather(output_squares, "tok", axis=1, tiled=True)
    own_square = lax.all_to_all(every_square, "feat", split_axis=1, concat_axis=0, tiled=True)
    own_square = jnp.roll(own_square, -place * activations.shape[0], axis=0)
    summed = lax.dot_general(
        all_inputs * all_inputs,
        own_square,
        (((0,), (0,)), ((), ())),
        precision=lax.Precision.HIGH,
        preferred_element_type=jnp.float32,
    )
    return summed / total_tokens


def solution(mesh):
    count, feats = mesh.shape["tok"], mesh.shape["feat"]
    in_specs = (P("tok", "feat"), P("tok", "feat"), P("feat", "tok"), P("feat", "tok"))
    out_specs = P("tok", "feat")

    def body(*args):
        return per_device(count, feats, *args)

    return jax.shard_map(body, mesh=mesh, in_specs=in_specs, out_specs=out_specs, check_vma=False)
```
